1024 devices in a mesh: row: 32 (over z_hi, y), col: 32 (over x, z_lo, core).
Axes of the slice: x: 4, y: 8, z: 16 (z_hi: 4, z_lo: 4; z = z_hi * 4 + z_lo), core: 2. Of those that a mesh axis runs over, the one named last changes fastest.
Arguments:
- vectors: bfloat16 [65536, 32], P(('col', 'row')), may hold values from -6 to 6
- row_degree: float32 [65536], P('row'), may hold values from 1 to 16
- col_degree: float32 [65536], P('col'), may hold values from 1 to 16
- tiles: bfloat16 [32, 32, 16, 256, 256], P('row', 'col'), may hold values from 0 to 0.029907227
- tile_rows: int32 [32, 32, 16], P('row', 'col'), may hold values from 0 to 7
- tile_cols: int32 [32, 32, 16], P('row', 'col'), may hold values from 0 to 7
- tile_counts: int32 [32, 32], P('row', 'col'), may hold values from 1 to 16, as said below
- lent_tiles: bfloat16 [32, 32, 8, 256, 256], P('row', 'col'), may hold values from 0 to 0.029907227
- lent_rows: int32 [32, 32, 8], P('row', 'col'), may hold values from 0 to 7
- lent_cols: int32 [32, 32, 8], P('row', 'col'), may hold values from 0 to 7
- lent_counts: int32 [32, 32], P('row', 'col'), may hold values from 0 to 8, as said below
Outputs:
- first: float32 [65536, 32], P(('row', 'col'))
- second: float32 [65536, 32], P(('col', 'row'))
The draws below stay inside these ranges and needn't reach their ends.
Inputs may be any that keep to these rules, and one draw needn't show every extreme that they name: `tile_counts`: in every tile-row block at least one block uses all 16 own slots; most use far fewer. `lent_counts`: in every tile-row block exactly one device holds 8 used borrowed slots: it is the partner (column XOR 16) of one block of that row that uses all 16 own slots (other blocks of the row may also use 16); all other counts are 0.
All inputs are finite; a program needn't handle non-finite values.
Results may differ from the reference program's by a relative error of at most 0.0033.
Values may be sent and summed in bfloat16 or wider, within the bound.
No kernel may reach another device: no remote copies, remote signals or barrier semaphores. Data moves between devices by JAX's collectives and lax.ppermute only.
A program may use at most 32 MiB of HBM per device.

```python
import math
import jax
import jax.numpy as jnp
import numpy as np
from jax import lax

TILE = 256
K = 32
SLOTS = 16
LENT = 8
NODES = 65536
RT = 8
CT = 8
RBLOCKS = 32
CBLOCKS = 32


def count_pair(key):
    inner = jax.random.fold_in(key, 21)
    base = jax.random.randint(jax.random.fold_in(inner, 1), (RBLOCKS, CBLOCKS), 1, SLOTS + 1)
    counts = jnp.maximum(1, base * base // SLOTS)
    heavy = jax.random.randint(jax.random.fold_in(inner, 2), (RBLOCKS,), 0, CBLOCKS)
    partner = jnp.bitwise_xor(heavy, CBLOCKS // 2)
    columns = jnp.arange(CBLOCKS, dtype=jnp.int32)
    is_heavy = columns[None, :] == heavy[:, None]
    is_partner = columns[None, :] == partner[:, None]
    counts = jnp.where(is_heavy, SLOTS, counts)
    counts = jnp.where(is_partner, jnp.minimum(counts, max(1, SLOTS // 4)), counts)
    lent = jnp.where(is_partner, LENT, 0)
    return (counts.astype(jnp.int32), lent.astype(jnp.int32))


def draw_tile_counts(key, part):
    return count_pair(key)[0]


def draw_lent_counts(key, part):
    return count_pair(key)[1]


def touch_ends(values, stream_key, smallest, high):
    spot = [jax.random.randint(jax.random.fold_in(stream_key, axis), (), 0, length) for axis, length in enumerate(values.shape)]
    longest = values.shape.index(max(values.shape))
    next_to = spot[:longest] + [(spot[longest] + 1) % values.shape[longest]] + spot[longest + 1:]
    return values.at[tuple(spot)].set(smallest).at[tuple(next_to)].set(high)


def shard_levels(stream_key, shape, pieces, low, high):
    loudness = 1.0
    for axis_at, shards_of in pieces:
        draws = jax.random.uniform(jax.random.fold_in(jax.random.fold_in(stream_key, 6), axis_at), (shards_of,), jnp.float32, low / len(pieces), high / len(pieces))
        loudness = loudness * jnp.repeat(jnp.exp(draws), shape[axis_at] // shards_of).reshape((-1,) + (1,) * (len(shape) - 1 - axis_at))
    return loudness


def rank_table(number_of, slope):
    weights = [(1 << 20) // math.isqrt(standing ** slope) + 1 for standing in range(1, number_of + 1)]
    scale = 1 + sum(weights) // (1 << 30)
    return np.cumsum(np.array([max(1, weight // scale) for weight in weights]))


def ranked(own_key, dims, amount, lean):
    grid = rank_table(amount, lean)
    ticket = jax.random.randint(jax.random.fold_in(own_key, 1), dims, 0, int(grid[amount - 1]))
    grade = jnp.searchsorted(jnp.asarray(grid, jnp.int32), ticket, side="right")
    return jax.random.permutation(jax.random.fold_in(own_key, 2), amount)[grade].astype(jnp.int32)


def scatter_about(stream_key, shape, deviation, limit, split=(), kind=jnp.bfloat16):
    result = deviation * jax.random.normal(stream_key, shape, jnp.float32)
    if split:
        result = result * shard_levels(stream_key, shape, split, -0.22, 0.18)
    return jnp.clip(result, -limit, limit).astype(kind)


def setup_inputs(seed: int = 0) -> dict:
    streams_of = jax.random.split(jax.random.key(seed), 12)
    vectors = scatter_about(streams_of[0], (NODES, K), 1.0, 6.0, ((0, 1024),))
    row_degree = jnp.clip(jnp.exp(math.log(16.0) - 2.7725887 * jax.random.uniform(streams_of[1], (NODES,), jnp.float32) ** shard_levels(streams_of[1], (NODES,), ((0, 32),), -0.2, 0.2)), 1.0, 16.0)
    col_degree = jnp.clip(jnp.exp(math.log(16.0) - 2.7725887 * jax.random.uniform(streams_of[2], (NODES,), jnp.float32) ** shard_levels(streams_of[2], (NODES,), ((0, 32),), -0.2, 0.2)), 1.0, 16.0)
    tiles = jnp.clip(0.029907227 * jax.random.uniform(streams_of[3], (RBLOCKS, CBLOCKS, SLOTS, TILE, TILE), jnp.float32) ** shard_levels(streams_of[3], (RBLOCKS, CBLOCKS, SLOTS, TILE, TILE), ((0, 32), (1, 32)), -0.2, 0.2), 0.0, 0.029907227).astype(jnp.bfloat16)
    tile_rows = touch_ends(ranked(streams_of[4], (RBLOCKS, CBLOCKS, SLOTS), RT, 2), jax.random.fold_in(streams_of[4], 3), 0, RT - 1).astype(jnp.int32)
    tile_cols = touch_ends(jax.random.randint(streams_of[5], (RBLOCKS, CBLOCKS, SLOTS), 0, CT), jax.random.fold_in(streams_of[5], 1), 0, CT - 1).astype(jnp.int32)
    tile_counts = draw_tile_counts(jax.random.fold_in(streams_of[11], 71), 0)
    lent_tiles = jnp.clip(0.029907227 * jax.random.uniform(streams_of[7], (RBLOCKS, CBLOCKS, LENT, TILE, TILE), jnp.float32) ** shard_levels(streams_of[7], (RBLOCKS, CBLOCKS, LENT, TILE, TILE), ((0, 32), (1, 32)), -0.2, 0.2), 0.0, 0.029907227).astype(jnp.bfloat16)
    lent_rows = touch_ends(ranked(streams_of[8], (RBLOCKS, CBLOCKS, LENT), RT, 2), jax.random.fold_in(streams_of[8], 3), 0, RT - 1).astype(jnp.int32)
    lent_cols = touch_ends(jax.random.randint(streams_of[9], (RBLOCKS, CBLOCKS, LENT), 0, CT), jax.random.fold_in(streams_of[9], 1), 0, CT - 1).astype(jnp.int32)
    lent_counts = draw_lent_counts(jax.random.fold_in(streams_of[11], 71), 0)
    return dict(vectors=vectors, row_degree=row_degree, col_degree=col_degree, tiles=tiles, tile_rows=tile_rows, tile_cols=tile_cols, tile_counts=tile_counts, lent_tiles=lent_tiles, lent_rows=lent_rows, lent_cols=lent_cols, lent_counts=lent_counts)


def reference(vectors, row_degree, col_degree, tiles, tile_rows, tile_cols, tile_counts, lent_tiles, lent_rows, lent_cols, lent_counts):
    rblocks, cblocks, slots, tile, _ = tiles.shape
    lent = lent_tiles.shape[2]
    width = vectors.shape[1]
    nodes = vectors.shape[0]
    row_tiles = nodes // (rblocks * tile)
    col_tiles = nodes // (cblocks * tile)
    half = cblocks // 2
    live = (jnp.arange(slots, dtype=jnp.int32)[None, None, :] < tile_counts[:, :, None]).astype(jnp.float32)
    live_lent = (jnp.arange(lent, dtype=jnp.int32)[None, None, :] < lent_counts[:, :, None]).astype(jnp.float32)
    scaled = (vectors.astype(jnp.float32) * lax.rsqrt(col_degree)[:, None]).astype(jnp.bfloat16)
    source = scaled.astype(jnp.float32).reshape(cblocks, col_tiles, tile, width)
    owner_col = jnp.bitwise_xor(jnp.arange(cblocks, dtype=jnp.int32), jnp.int32(half))

    def first_block(i):
        block_tiles = tiles[i].astype(jnp.float32)
        picked = source[jnp.arange(cblocks)[:, None], tile_cols[i]]
        prod = jnp.einsum('csab,csbk->csak', block_tiles, picked)
        place = (tile_rows[i][:, :, None] == jnp.arange(row_tiles, dtype=jnp.int32)).astype(jnp.float32) * live[i][:, :, None]
        total = jnp.einsum('cst,csak->tak', place, prod)
        borrowed = lent_tiles[i].astype(jnp.float32)
        picked_lent = source[owner_col[:, None], lent_cols[i]]
        prod_lent = jnp.einsum('csab,csbk->csak', borrowed, picked_lent)
        place_lent = (lent_rows[i][:, :, None] == jnp.arange(row_tiles, dtype=jnp.int32)).astype(jnp.float32) * live_lent[i][:, :, None]
        return total + jnp.einsum('cst,csak->tak', place_lent, prod_lent)
    part_one = lax.map(first_block, jnp.arange(rblocks, dtype=jnp.int32))
    first = part_one.reshape(nodes, width) * lax.rsqrt(row_degree)[:, None]
    middle = first.astype(jnp.bfloat16).astype(jnp.float32).reshape(rblocks, row_tiles, tile, width)

    def second_block(j):
        block_tiles = tiles[:, j].astype(jnp.float32)
        picked = middle[jnp.arange(rblocks)[:, None], tile_rows[:, j]]
        prod = jnp.einsum('rsab,rsak->rsbk', block_tiles, picked)
        place = (tile_cols[:, j][:, :, None] == jnp.arange(col_tiles, dtype=jnp.int32)).astype(jnp.float32) * live[:, j][:, :, None]
        total = jnp.einsum('rst,rsbk->tbk', place, prod)
        holder = jnp.bitwise_xor(j, jnp.int32(half))
        borrowed = lent_tiles[:, holder].astype(jnp.float32)
        picked_lent = middle[jnp.arange(rblocks)[:, None], lent_rows[:, holder]]
        prod_lent = jnp.einsum('rsab,rsak->rsbk', borrowed, picked_lent)
        place_lent = (lent_cols[:, holder][:, :, None] == jnp.arange(col_tiles, dtype=jnp.int32)).astype(jnp.float32) * live_lent[:, holder][:, :, None]
        return total + jnp.einsum('rst,rsbk->tbk', place_lent, prod_lent)
    part_two = lax.map(second_block, jnp.arange(cblocks, dtype=jnp.int32))
    second = part_two.reshape(nodes, width) * lax.rsqrt(col_degree)[:, None]
    return (first, second)
```

```python
import jax
import jax.numpy as jnp
from jax import lax
from jax.experimental import pallas as pl
from jax.experimental.pallas import tpu as pltpu
from jax.sharding import PartitionSpec as P

GROUP = 4
F32 = jnp.float32
BF16 = jnp.bfloat16


def vmem():
    return pl.BlockSpec(memory_space=pltpu.VMEM)


def smem():
    return pl.BlockSpec(memory_space=pltpu.SMEM)


def any_space():
    return pl.BlockSpec(memory_space=pl.ANY)


def low_lanes(shape):
    return lax.broadcasted_iota(jnp.int32, shape, len(shape) - 1) < shape[-1] // 2


def shard_scale(degree_ref, place):
    line = degree_ref[pl.ds(place // 2, 1), :]
    turned = pltpu.roll(line, 64, 1)
    first_half = place % 2 == 0
    low = low_lanes(line.shape)
    both = jnp.where(low == first_half, line, turned)
    return lax.rsqrt(both)


def pack_kernel(place_ref, vectors_ref, degree_ref, out_ref):
    scale = shard_scale(degree_ref, place_ref[0])
    values = vectors_ref[...].astype(F32)
    half = values.shape[0] // 2
    wide = jnp.concatenate([values[:half], values[half:]], axis=1) * scale
    packed = wide.astype(BF16)
    for copy in range(out_ref.shape[0]):
        out_ref[copy] = packed


def unpack_source(source_ref, wide_ref):
    low = low_lanes((16, 128))
    for pair in range(source_ref.shape[0] // 2):
        even = source_ref[2 * pair].astype(F32)
        odd = source_ref[2 * pair + 1].astype(F32)
        top = jnp.where(low, even, pltpu.roll(odd, 64, 1))
        bottom = jnp.where(low, pltpu.roll(even, 64, 1), odd)
        lanes = slice(128 * (pair % 2), 128 * (pair % 2) + 128)
        wide_ref[pair // 2, 0:16, lanes] = top.astype(BF16)
        wide_ref[pair // 2, 16:32, lanes] = bottom.astype(BF16)


def pack_total(total_ref, out_ref):
    low = low_lanes((16, 128))
    for pair in range(out_ref.shape[0] // 2):
        lanes = slice(128 * (pair % 2), 128 * (pair % 2) + 128)
        top = total_ref[pair // 2, 0:16, lanes]
        bottom = total_ref[pair // 2, 16:32, lanes]
        even = jnp.where(low, top, pltpu.roll(bottom, 64, 1))
        odd = jnp.where(low, pltpu.roll(top, 64, 1), bottom)
        out_ref[2 * pair] = even.astype(out_ref.dtype)
        out_ref[2 * pair + 1] = odd.astype(out_ref.dtype)


def tile_copy(tiles_ref, buffer_ref, sems, slot):
    return pltpu.make_async_copy(tiles_ref.at[slot], buffer_ref.at[slot], sems.at[slot])


def start_tiles(tiles_ref, buffer_ref, sems, groups):
    def start(slot, carry):
        tile_copy(tiles_ref, buffer_ref, sems, slot).start()
        return carry

    lax.fori_loop(0, groups * GROUP, start, 0)


def add_tiles(table_ref, at_in, at_out, used, groups, wide_ref, total_ref, tiles_ref, buffer_ref, sems, flip):
    contract = (((1,), (0,)), ((), ())) if flip else (((1,), (1,)), ((), ()))

    def body(group, carry):
        base = group * GROUP
        prods = []
        for lane in range(GROUP):
            slot = base + lane
            tile_copy(tiles_ref, buffer_ref, sems, slot).wait()
            source = wide_ref[table_ref[at_in + slot]]
            prod = lax.dot_general(
                source, buffer_ref[slot], contract, preferred_element_type=F32
            )
            prods.append(jnp.where(slot < used, prod, 0.0))
        for lane in range(GROUP):
            spot = table_ref[at_out + base + lane]
            total_ref[spot] = total_ref[spot] + prods[lane]
        return carry

    lax.fori_loop(0, groups, body, 0)


def product_kernel(at_in, at_out, at_used, flip, packed, seeded):
    def kernel(*refs):
        if seeded:
            table_ref, source_ref, tiles_ref, seed_ref, out_ref = refs[:5]
        else:
            table_ref, source_ref, tiles_ref, out_ref = refs[:4]
        wide_ref, total_scratch, buffer_ref, sems = refs[-4:]
        used = table_ref[at_used]
        groups = (used + GROUP - 1) // GROUP
        start_tiles(tiles_ref, buffer_ref, sems, groups)
        total_ref = total_scratch if packed else out_ref
        if seeded:
            total_ref[...] = seed_ref[...]
        else:
            total_ref[...] = jnp.zeros_like(total_ref)

        @pl.when(used > 0)
        def _():
            unpack_source(source_ref, wide_ref)

        add_tiles(
            table_ref, at_in, at_out, used, groups, wide_ref, total_ref, tiles_ref, buffer_ref, sems, flip
        )
        if packed:
            pack_total(total_ref, out_ref)

    return kernel


def product(table, source, tiles, at_in, at_out, at_used, flip, out_dtype=None, seed=None):
    slots = tiles.shape[0]
    chunks = source.shape[0]
    wide = (chunks // 4, 32, 256)
    packed = out_dtype is not None
    out = (
        jax.ShapeDtypeStruct((chunks, 16, 128), out_dtype)
        if packed
        else jax.ShapeDtypeStruct(wide, F32)
    )
    seeds = [] if seed is None else [seed]
    return pl.pallas_call(
        product_kernel(at_in, at_out, at_used, flip, packed, seed is not None),
        out_shape=out,
        in_specs=[smem(), vmem(), any_space()] + [vmem()] * len(seeds),
        out_specs=vmem(),
        scratch_shapes=[
            pltpu.VMEM(wide, BF16),
            pltpu.VMEM(wide if packed else (1, 8, 128), F32),
            pltpu.VMEM(tiles.shape, tiles.dtype),
            pltpu.SemaphoreType.DMA((slots,)),
        ],
    )(table, source, tiles, *seeds)


def sum_chunks(received_ref):
    parts = [received_ref[chunk].astype(F32) for chunk in range(received_ref.shape[0])]
    while len(parts) > 1:
        parts = [parts[k] + parts[k + 1] for k in range(0, len(parts), 2)]
    return parts[0]


def store_shard(out_ref, wide):
    out_ref[0:16, :] = wide[:, 0:64]
    out_ref[16:32, :] = pltpu.roll(wide, 64, 1)[:, 0:64]


def middle_kernel(place_ref, received_ref, degree_ref, out_ref, copies_ref):
    wide = sum_chunks(received_ref) * shard_scale(degree_ref, place_ref[1])
    store_shard(out_ref, wide)
    packed = wide.astype(BF16)
    for copy in range(copies_ref.shape[0]):
        copies_ref[copy] = packed


def last_kernel(place_ref, received_ref, degree_ref, out_ref):
    wide = sum_chunks(received_ref) * shard_scale(degree_ref, place_ref[0])
    store_shard(out_ref, wide)


def exchange(chunks, axis):
    return lax.all_to_all(chunks, axis, 0, 0, tiled=True)


def partner(block):
    count = lax.axis_size("col")
    return lax.ppermute(block, "col", [(k, k ^ (count // 2)) for k in range(count)])


def shards(
    vectors,
    row_degree,
    col_degree,
    tiles,
    tile_rows,
    tile_cols,
    tile_counts,
    lent_tiles,
    lent_rows,
    lent_cols,
    lent_counts,
):
    own = tiles.reshape(tiles.shape[2:])
    lent = lent_tiles.reshape(lent_tiles.shape[2:])
    slots, lents = own.shape[0], lent.shape[0]
    table = jnp.concatenate(
        [
            tile_rows.reshape(-1),
            tile_cols.reshape(-1),
            lent_rows.reshape(-1),
            lent_cols.reshape(-1),
            tile_counts.reshape(-1),
            lent_counts.reshape(-1),
        ]
    )
    at_rows, at_cols = 0, slots
    at_lent_rows, at_lent_cols = 2 * slots, 2 * slots + lents
    at_used, at_lent_used = 2 * slots + 2 * lents, 2 * slots + 2 * lents + 1
    place = jnp.stack([lax.axis_index("row"), lax.axis_index("col")]).astype(jnp.int32)
    row_lines = row_degree.reshape(-1, 128)
    col_lines = col_degree.reshape(-1, 128)
    row_size, col_size = lax.axis_size("row"), lax.axis_size("col")

    copies = pl.pallas_call(
        pack_kernel,
        out_shape=jax.ShapeDtypeStruct((row_size, 16, 128), BF16),
        in_specs=[smem(), vmem(), vmem()],
        out_specs=vmem(),
    )(place, vectors.T, col_lines)
    source = exchange(copies, "row")
    lent_source = partner(source)
    total = product(table, source, own, at_cols, at_rows, at_used, False)
    partial_value = product(
        table, lent_source, lent, at_lent_cols, at_lent_rows, at_lent_used, False, BF16, total
    )
    first, middle_copies = pl.pallas_call(
        middle_kernel,
        out_shape=(
            jax.ShapeDtypeStruct((32, 64), F32),
            jax.ShapeDtypeStruct((col_size, 16, 128), BF16),
        ),
        in_specs=[smem(), vmem(), vmem()],
        out_specs=(vmem(), vmem()),
    )(place, exchange(partial_value, "col"), row_lines)
    middle = exchange(middle_copies, "col")
    lent_back = product(
        table, middle, lent, at_lent_rows, at_lent_cols, at_lent_used, True, BF16
    )
    home_back = partner(lent_back)
    own_back = product(table, middle, own, at_rows, at_cols, at_used, True, F32)
    partial_back = (own_back + home_back.astype(F32)).astype(BF16)
    second = pl.pallas_call(
        last_kernel,
        out_shape=jax.ShapeDtypeStruct((32, 64), F32),
        in_specs=[smem(), vmem(), vmem()],
        out_specs=vmem(),
    )(place, exchange(partial_back, "row"), col_lines)
    return (first.T, second.T)


def solution(mesh):
    return jax.shard_map(
        shards,
        mesh=mesh,
        in_specs=(
            P(("col", "row"), None),
            P("row"),
            P("col"),
            P("row", "col", None, None, None),
            P("row", "col", None),
            P("row", "col", None),
            P("row", "col"),
            P("row", "col", None, None, None),
            P("row", "col", None),
            P("row", "col", None),
            P("row", "col"),
        ),
        out_specs=(P(("row", "col"), None), P(("col", "row"), None)),
        check_vma=False,
    )
```

```python
import jax
import jax.numpy as jnp
from jax import lax
from jax.experimental import pallas as pl
from jax.experimental.pallas import tpu as pltpu
from jax.sharding import PartitionSpec as P

GROUP = 4
F32 = jnp.float32
BF16 = jnp.bfloat16


def vmem():
    return pl.BlockSpec(memory_space=pltpu.VMEM)


def smem():
    return pl.BlockSpec(memory_space=pltpu.SMEM)


def any_space():
    return pl.BlockSpec(memory_space=pl.ANY)


def OUT(shape, dtype):
    return pltpu.VMEM(shape, dtype)


def near(array):
    return pltpu.with_memory_space_constraint(array, pltpu.VMEM)


def low_lanes(shape):
    return lax.broadcasted_iota(jnp.int32, shape, len(shape) - 1) < shape[-1] // 2


def shard_scale(degree_ref, place):
    line = degree_ref[pl.ds(place // 2, 1), :]
    turned = pltpu.roll(line, 64, 1)
    first_half = place % 2 == 0
    low = low_lanes(line.shape)
    both = jnp.where(low == first_half, line, turned)
    return lax.rsqrt(both)


def pack_kernel(vectors_ref, degree_ref, out_ref):
    scale = shard_scale(degree_ref, lax.axis_index("row"))
    values = vectors_ref[...].astype(F32)
    half = values.shape[0] // 2
    wide = jnp.concatenate([values[:half], values[half:]], axis=1) * scale
    packed = wide.astype(BF16)
    for copy in range(out_ref.shape[0]):
        out_ref[copy] = packed


def unpack_source(source_ref, wide_ref):
    low = low_lanes((16, 128))
    for pair in range(source_ref.shape[0] // 2):
        even = source_ref[2 * pair].astype(F32)
        odd = source_ref[2 * pair + 1].astype(F32)
        top = jnp.where(low, even, pltpu.roll(odd, 64, 1))
        bottom = jnp.where(low, pltpu.roll(even, 64, 1), odd)
        lanes = slice(128 * (pair % 2), 128 * (pair % 2) + 128)
        wide_ref[pair // 2, 0:16, lanes] = top.astype(BF16)
        wide_ref[pair // 2, 16:32, lanes] = bottom.astype(BF16)


def pack_total(total_ref, out_ref):
    low = low_lanes((16, 128))
    for pair in range(out_ref.shape[0] // 2):
        lanes = slice(128 * (pair % 2), 128 * (pair % 2) + 128)
        top = total_ref[pair // 2, 0:16, lanes]
        bottom = total_ref[pair // 2, 16:32, lanes]
        even = jnp.where(low, top, pltpu.roll(bottom, 64, 1))
        odd = jnp.where(low, pltpu.roll(top, 64, 1), bottom)
        out_ref[2 * pair] = even.astype(out_ref.dtype)
        out_ref[2 * pair + 1] = odd.astype(out_ref.dtype)


def group_count(used):
    return (used + GROUP - 1) // GROUP


def tile_copy(tiles_ref, buffer_ref, sems, slot):
    return pltpu.make_async_copy(tiles_ref.at[slot], buffer_ref.at[slot], sems.at[slot])


def start_tiles(tiles_ref, buffer_ref, sems, used):
    def start(slot, carry):
        tile_copy(tiles_ref, buffer_ref, sems, slot).start()
        return carry

    lax.fori_loop(0, group_count(used) * GROUP, start, 0)


def add_tiles(in_at, out_at, used, wide_ref, total_ref, buffer_ref, flip, wait=None):
    contract = (((1,), (0,)), ((), ())) if flip else (((1,), (1,)), ((), ()))

    def body(group, carry):
        base = group * GROUP
        prods = []
        for step in range(GROUP):
            slot = base + step
            if wait is not None:
                wait(slot)
            prod = lax.dot_general(
                wide_ref[in_at(slot)], buffer_ref[slot], contract, preferred_element_type=F32
            )
            prods.append(jnp.where(slot < used, prod, 0.0))
        for step in range(GROUP):
            spot = out_at(base + step)
            total_ref[spot] = total_ref[spot] + prods[step]
        return carry

    lax.fori_loop(0, group_count(used), body, 0)


def own_kernel(
    rows_ref, cols_ref, count_ref, source_ref, tiles_ref, total_ref, wide_out_ref, buffer_ref, sems
):
    used = count_ref[0, 0]
    start_tiles(tiles_ref, buffer_ref, sems, used)
    total_ref[...] = jnp.zeros_like(total_ref)
    unpack_source(source_ref, wide_out_ref)
    add_tiles(
        lambda slot: cols_ref[0, 0, slot],
        lambda slot: rows_ref[0, 0, slot],
        used,
        wide_out_ref,
        total_ref,
        buffer_ref,
        False,
        lambda slot: tile_copy(tiles_ref, buffer_ref, sems, slot).wait(),
    )


def home_kernel(index_ref, wide_ref, home_ref, total_ref, out_ref, sum_ref):
    sum_ref[...] = total_ref[...]
    add_tiles(
        lambda slot: index_ref[1, slot],
        lambda slot: index_ref[0, slot],
        index_ref[2, 0],
        wide_ref,
        sum_ref,
        home_ref,
        False,
    )
    pack_total(sum_ref, out_ref)


def back_kernel(
    rows_ref,
    cols_ref,
    count_ref,
    index_ref,
    source_ref,
    tiles_ref,
    home_ref,
    out_ref,
    wide_ref,
    sum_ref,
    buffer_ref,
    sems,
):
    used = count_ref[0, 0]
    start_tiles(tiles_ref, buffer_ref, sems, used)
    sum_ref[...] = jnp.zeros_like(sum_ref)
    unpack_source(source_ref, wide_ref)
    add_tiles(
        lambda slot: rows_ref[0, 0, slot],
        lambda slot: cols_ref[0, 0, slot],
        used,
        wide_ref,
        sum_ref,
        buffer_ref,
        True,
        lambda slot: tile_copy(tiles_ref, buffer_ref, sems, slot).wait(),
    )
    add_tiles(
        lambda slot: index_ref[0, slot],
        lambda slot: index_ref[1, slot],
        index_ref[2, 0],
        wide_ref,
        sum_ref,
        home_ref,
        True,
    )
    pack_total(sum_ref, out_ref)


def sum_chunks(received_ref):
    parts = [received_ref[chunk].astype(F32) for chunk in range(received_ref.shape[0])]
    while len(parts) > 1:
        parts = [parts[k] + parts[k + 1] for k in range(0, len(parts), 2)]
    return parts[0]


def store_shard(out_ref, wide):
    out_ref[0:16, :] = wide[:, 0:64]
    out_ref[16:32, :] = pltpu.roll(wide, 64, 1)[:, 0:64]


def middle_kernel(received_ref, degree_ref, out_ref, copies_ref):
    wide = sum_chunks(received_ref) * shard_scale(degree_ref, lax.axis_index("col"))
    store_shard(out_ref, wide)
    packed = wide.astype(BF16)
    for copy in range(copies_ref.shape[0]):
        copies_ref[copy] = packed


def last_kernel(received_ref, degree_ref, out_ref):
    wide = sum_chunks(received_ref) * shard_scale(degree_ref, lax.axis_index("row"))
    store_shard(out_ref, wide)


def exchange(chunks, axis):
    return lax.all_to_all(chunks, axis, 0, 0, tiled=True)


def partner(block):
    count = lax.axis_size("col")
    return lax.ppermute(block, "col", [(k, k ^ (count // 2)) for k in range(count)])


def shards(
    vectors,
    row_degree,
    col_degree,
    tiles,
    tile_rows,
    tile_cols,
    tile_counts,
    lent_tiles,
    lent_rows,
    lent_cols,
    lent_counts,
):
    own = tiles.reshape(tiles.shape[2:])
    lent = lent_tiles.reshape(lent_tiles.shape[2:])
    slots, lents = own.shape[0], lent.shape[0]
    row_lines = row_degree.reshape(-1, 128)
    col_lines = col_degree.reshape(-1, 128)
    row_size, col_size = lax.axis_size("row"), lax.axis_size("col")
    chunk = (16, 128)
    wide = (row_degree.shape[0] // 256, 32, 256)

    index = jnp.stack(
        [
            lent_rows.reshape(-1),
            lent_cols.reshape(-1),
            jnp.broadcast_to(lent_counts.reshape(1), (lents,)),
        ]
    )
    home = near(partner(lent))
    home_index = partner(index)
    copies = pl.pallas_call(
        pack_kernel,
        out_shape=OUT((row_size,) + chunk, BF16),
        in_specs=[vmem(), vmem()],
        out_specs=vmem(),
    )(vectors.T, col_lines)
    source = exchange(copies, "row")
    total, wide_source = pl.pallas_call(
        own_kernel,
        out_shape=(OUT(wide, F32), OUT(wide, BF16)),
        in_specs=[smem(), smem(), smem(), vmem(), any_space()],
        out_specs=(vmem(), vmem()),
        scratch_shapes=[
            pltpu.VMEM(own.shape, BF16),
            pltpu.SemaphoreType.DMA((slots,)),
        ],
    )(tile_rows, tile_cols, tile_counts, near(source), own)
    partial_value = pl.pallas_call(
        home_kernel,
        out_shape=OUT((col_size,) + chunk, BF16),
        in_specs=[smem(), vmem(), vmem(), vmem()],
        out_specs=vmem(),
        scratch_shapes=[pltpu.VMEM(wide, F32)],
    )(home_index, near(wide_source), home, near(total))
    first, middle_copies = pl.pallas_call(
        middle_kernel,
        out_shape=(OUT((32, 64), F32), OUT((col_size,) + chunk, BF16)),
        in_specs=[vmem(), vmem()],
        out_specs=(vmem(), vmem()),
    )(near(exchange(partial_value, "col")), row_lines)
    middle = exchange(middle_copies, "col")
    partial_back = pl.pallas_call(
        back_kernel,
        out_shape=OUT((row_size,) + chunk, BF16),
        in_specs=[smem(), smem(), smem(), smem(), vmem(), any_space(), vmem()],
        out_specs=vmem(),
        scratch_shapes=[
            pltpu.VMEM(wide, BF16),
            pltpu.VMEM(wide, F32),
            pltpu.VMEM(own.shape, BF16),
            pltpu.SemaphoreType.DMA((slots,)),
        ],
    )(tile_rows, tile_cols, tile_counts, home_index, near(middle), own, home)
    second = pl.pallas_call(
        last_kernel,
        out_shape=jax.ShapeDtypeStruct((32, 64), F32),
        in_specs=[vmem(), vmem()],
        out_specs=vmem(),
    )(near(exchange(partial_back, "row")), col_lines)
    return (first.T, second.T)


def solution(mesh):
    return jax.shard_map(
        shards,
        mesh=mesh,
        in_specs=(
            P(("col", "row"), None),
            P("row"),
            P("col"),
            P("row", "col", None, None, None),
            P("row", "col", None),
            P("row", "col", None),
            P("row", "col"),
            P("row", "col", None, None, None),
            P("row", "col", None),
            P("row", "col", None),
            P("row", "col"),
        ),
        out_specs=(P(("row", "col"), None), P(("col", "row"), None)),
        check_vma=False,
    )
```

```python
import jax
import jax.numpy as jnp
from jax import lax
from jax.experimental import pallas as pl
from jax.experimental.pallas import tpu as pltpu
from jax.sharding import PartitionSpec as P

GROUP = 8
SMALL = pltpu.CompilerParams(vmem_limit_bytes=4 * 1024 * 1024)
F32 = jnp.float32
BF16 = jnp.bfloat16


def vmem():
    return pl.BlockSpec(memory_space=pltpu.VMEM)


def smem():
    return pl.BlockSpec(memory_space=pltpu.SMEM)


def OUT(shape, dtype):
    return pltpu.VMEM(shape, dtype)


def near(array):
    return pltpu.with_memory_space_constraint(array, pltpu.VMEM)


def far(array):
    return pltpu.with_memory_space_constraint(array, pltpu.HBM)


def low_lanes(shape):
    return lax.broadcasted_iota(jnp.int32, shape, len(shape) - 1) < shape[-1] // 2


def shard_scale(degree_ref, place):
    line = degree_ref[pl.ds(place // 2, 1), :]
    turned = pltpu.roll(line, 64, 1)
    first_half = place % 2 == 0
    low = low_lanes(line.shape)
    both = jnp.where(low == first_half, line, turned)
    return lax.rsqrt(both)


def pack_kernel(vectors_ref, degree_ref, out_ref):
    scale = shard_scale(degree_ref, lax.axis_index("row"))
    values = vectors_ref[...].astype(F32)
    half = values.shape[0] // 2
    wide = jnp.concatenate([values[:half], values[half:]], axis=1) * scale
    packed = wide.astype(BF16)
    for copy in range(out_ref.shape[0]):
        out_ref[copy] = packed


def unpack_source(source_ref, wide_ref):
    low = low_lanes((16, 128))
    for pair in range(source_ref.shape[0] // 2):
        even = source_ref[2 * pair].astype(F32)
        odd = source_ref[2 * pair + 1].astype(F32)
        top = jnp.where(low, even, pltpu.roll(odd, 64, 1))
        bottom = jnp.where(low, pltpu.roll(even, 64, 1), odd)
        lanes = slice(128 * (pair % 2), 128 * (pair % 2) + 128)
        wide_ref[pair // 2, 0:16, lanes] = top.astype(BF16)
        wide_ref[pair // 2, 16:32, lanes] = bottom.astype(BF16)


def pack_total(total_ref, out_ref):
    low = low_lanes((16, 128))
    for pair in range(out_ref.shape[0] // 2):
        lanes = slice(128 * (pair % 2), 128 * (pair % 2) + 128)
        top = total_ref[pair // 2, 0:16, lanes]
        bottom = total_ref[pair // 2, 16:32, lanes]
        even = jnp.where(low, top, pltpu.roll(bottom, 64, 1))
        odd = jnp.where(low, pltpu.roll(top, 64, 1), bottom)
        out_ref[2 * pair] = even.astype(out_ref.dtype)
        out_ref[2 * pair + 1] = odd.astype(out_ref.dtype)


def add_tiles(in_at, out_at, used, wide_ref, total_ref, tiles_ref, flip):
    contract = (((1,), (0,)), ((), ())) if flip else (((1,), (1,)), ((), ()))

    def body(group, carry):
        base = group * GROUP
        prods = []
        for step in range(GROUP):
            slot = base + step
            prod = lax.dot_general(
                wide_ref[in_at(slot)], tiles_ref[slot], contract, preferred_element_type=F32
            )
            prods.append(jnp.where(slot < used, prod, 0.0))
        for step in range(GROUP):
            spot = out_at(base + step)
            total_ref[spot] = total_ref[spot] + prods[step]
        return carry

    lax.fori_loop(0, (used + GROUP - 1) // GROUP, body, 0)


def product_kernel(flip):
    def kernel(
        rows_ref, cols_ref, count_ref, index_ref, source_ref, tiles_ref, home_ref, out_ref, wide_ref, sum_ref
    ):
        sum_ref[...] = jnp.zeros_like(sum_ref)
        unpack_source(source_ref, wide_ref)
        own_row = lambda slot: rows_ref[0, 0, slot]
        own_col = lambda slot: cols_ref[0, 0, slot]
        home_row = lambda slot: index_ref[0, slot]
        home_col = lambda slot: index_ref[1, slot]
        if flip:
            own_in, own_out, home_in, home_out = own_row, own_col, home_row, home_col
        else:
            own_in, own_out, home_in, home_out = own_col, own_row, home_col, home_row
        add_tiles(own_in, own_out, count_ref[0, 0], wide_ref, sum_ref, tiles_ref, flip)
        add_tiles(home_in, home_out, index_ref[2, 0], wide_ref, sum_ref, home_ref, flip)
        pack_total(sum_ref, out_ref)

    return kernel


def product(rows, cols, count, index, source, tiles, home, flip):
    wide = (source.shape[0] // 4, 32, 256)
    return pl.pallas_call(
        product_kernel(flip),
        compiler_params=SMALL,
        out_shape=OUT(source.shape, BF16),
        in_specs=[smem(), smem(), smem(), smem(), vmem(), vmem(), vmem()],
        out_specs=vmem(),
        scratch_shapes=[pltpu.VMEM(wide, BF16), pltpu.VMEM(wide, F32)],
    )(rows, cols, count, index, near(source), near(tiles), home)


def load_kernel(tiles_ref, out_ref, sem):
    copy = pltpu.make_async_copy(tiles_ref, out_ref, sem)
    copy.start()
    copy.wait()


def load_tiles(tiles):
    return pl.pallas_call(
        load_kernel,
        compiler_params=SMALL,
        out_shape=OUT(tiles.shape, tiles.dtype),
        in_specs=[pl.BlockSpec(memory_space=pl.ANY)],
        out_specs=vmem(),
        scratch_shapes=[pltpu.SemaphoreType.DMA],
    )(tiles)


def sum_chunks(received_ref):
    parts = [received_ref[chunk].astype(F32) for chunk in range(received_ref.shape[0])]
    while len(parts) > 1:
        parts = [parts[k] + parts[k + 1] for k in range(0, len(parts), 2)]
    return parts[0]


def store_shard(out_ref, wide):
    out_ref[0:16, :] = wide[:, 0:64]
    out_ref[16:32, :] = pltpu.roll(wide, 64, 1)[:, 0:64]


def middle_kernel(received_ref, degree_ref, out_ref, copies_ref):
    wide = sum_chunks(received_ref) * shard_scale(degree_ref, lax.axis_index("col"))
    store_shard(out_ref, wide)
    packed = wide.astype(BF16)
    for copy in range(copies_ref.shape[0]):
        copies_ref[copy] = packed


def last_kernel(received_ref, degree_ref, out_ref):
    wide = sum_chunks(received_ref) * shard_scale(degree_ref, lax.axis_index("row"))
    store_shard(out_ref, wide)


def exchange(chunks, axis):
    return lax.all_to_all(chunks, axis, 0, 0, tiled=True)


def partner(block):
    count = lax.axis_size("col")
    return lax.ppermute(block, "col", [(k, k ^ (count // 2)) for k in range(count)])


def shards(
    vectors,
    row_degree,
    col_degree,
    tiles,
    tile_rows,
    tile_cols,
    tile_counts,
    lent_tiles,
    lent_rows,
    lent_cols,
    lent_counts,
):
    own = load_tiles(far(tiles.reshape(tiles.shape[2:])))
    lent = lent_tiles.reshape(lent_tiles.shape[2:])
    lents = lent.shape[0]
    tile_rows = far(tile_rows)
    tile_cols = far(tile_cols)
    row_lines = near(row_degree.reshape(-1, 128))
    col_lines = col_degree.reshape(-1, 128)
    row_size, col_size = lax.axis_size("row"), lax.axis_size("col")
    chunk = (16, 128)

    index = jnp.stack(
        [
            lent_rows.reshape(-1),
            lent_cols.reshape(-1),
            jnp.broadcast_to(lent_counts.reshape(1), (lents,)),
        ]
    )
    home = near(partner(lent))
    home_index = partner(index)
    copies = pl.pallas_call(
        pack_kernel,
        compiler_params=SMALL,
        out_shape=OUT((row_size,) + chunk, BF16),
        in_specs=[vmem(), vmem()],
        out_specs=vmem(),
    )(far(vectors.T), far(col_lines))
    source = exchange(copies, "row")
    partial_value = product(
        tile_rows, tile_cols, tile_counts, home_index, source, own, home, False
    )
    first, middle_copies = pl.pallas_call(
        middle_kernel,
        compiler_params=SMALL,
        out_shape=(OUT((32, 64), F32), OUT((col_size,) + chunk, BF16)),
        in_specs=[vmem(), vmem()],
        out_specs=(vmem(), vmem()),
    )(near(exchange(partial_value, "col")), row_lines)
    middle = exchange(middle_copies, "col")
    partial_back = product(
        tile_rows, tile_cols, tile_counts, home_index, middle, own, home, True
    )
    second = pl.pallas_call(
        last_kernel,
        compiler_params=SMALL,
        out_shape=jax.ShapeDtypeStruct((32, 64), F32),
        in_specs=[vmem(), vmem()],
        out_specs=vmem(),
    )(near(exchange(partial_back, "row")), near(col_lines))
    return (first.T, second.T)


def solution(mesh):
    return jax.shard_map(
        shards,
        mesh=mesh,
        in_specs=(
            P(("col", "row"), None),
            P("row"),
            P("col"),
            P("row", "col", None, None, None),
            P("row", "col", None),
            P("row", "col", None),
            P("row", "col"),
            P("row", "col", None, None, None),
            P("row", "col", None),
            P("row", "col", None),
            P("row", "col"),
        ),
        out_specs=(P(("row", "col"), None), P(("col", "row"), None)),
        check_vma=False,
    )
```

```python
import jax
import jax.numpy as jnp
from jax import lax
from jax.experimental import pallas as pl
from jax.experimental.pallas import tpu as pltpu
from jax.sharding import PartitionSpec as P

GROUP = 8
SMALL = pltpu.CompilerParams(vmem_limit_bytes=4 * 1024 * 1024)
F32 = jnp.float32
BF16 = jnp.bfloat16


def vmem():
    return pl.BlockSpec(memory_space=pltpu.VMEM)


def smem():
    return pl.BlockSpec(memory_space=pltpu.SMEM)


def OUT(shape, dtype):
    return pltpu.VMEM(shape, dtype)


def near(array):
    return pltpu.with_memory_space_constraint(array, pltpu.VMEM)


def far(array):
    return pltpu.with_memory_space_constraint(array, pltpu.HBM)


def low_lanes(shape):
    return lax.broadcasted_iota(jnp.int32, shape, len(shape) - 1) < shape[-1] // 2


def shard_scale(degree_ref, place):
    line = degree_ref[pl.ds(place // 2, 1), :]
    turned = pltpu.roll(line, 64, 1)
    first_half = place % 2 == 0
    low = low_lanes(line.shape)
    both = jnp.where(low == first_half, line, turned)
    return lax.rsqrt(both)


def pack_kernel(vectors_ref, degree_ref, out_ref):
    scale = shard_scale(degree_ref, lax.axis_index("row"))
    values = vectors_ref[...].astype(F32)
    half = values.shape[0] // 2
    wide = jnp.concatenate([values[:half], values[half:]], axis=1) * scale
    packed = wide.astype(BF16)
    for copy in range(out_ref.shape[0]):
        out_ref[copy] = packed


def unpack_source(source_ref, wide_ref):
    low = low_lanes((16, 128))
    for pair in range(source_ref.shape[0] // 2):
        even = source_ref[2 * pair].astype(F32)
        odd = source_ref[2 * pair + 1].astype(F32)
        top = jnp.where(low, even, pltpu.roll(odd, 64, 1))
        bottom = jnp.where(low, pltpu.roll(even, 64, 1), odd)
        lanes = slice(128 * (pair % 2), 128 * (pair % 2) + 128)
        wide_ref[pair // 2, 0:16, lanes] = top.astype(BF16)
        wide_ref[pair // 2, 16:32, lanes] = bottom.astype(BF16)


def pack_total(total_ref, out_ref):
    low = low_lanes((16, 128))
    for pair in range(out_ref.shape[0] // 2):
        lanes = slice(128 * (pair % 2), 128 * (pair % 2) + 128)
        top = total_ref[pair // 2, 0:16, lanes]
        bottom = total_ref[pair // 2, 16:32, lanes]
        even = jnp.where(low, top, pltpu.roll(bottom, 64, 1))
        odd = jnp.where(low, pltpu.roll(top, 64, 1), bottom)
        out_ref[2 * pair] = even.astype(out_ref.dtype)
        out_ref[2 * pair + 1] = odd.astype(out_ref.dtype)


def add_tiles(in_at, out_at, used, wide_ref, total_ref, tiles_ref, flip):
    contract = (((1,), (0,)), ((), ())) if flip else (((1,), (1,)), ((), ()))

    def body(group, carry):
        base = group * GROUP
        prods = []
        for step in range(GROUP):
            slot = base + step
            prod = lax.dot_general(
                wide_ref[in_at(slot)], tiles_ref[slot], contract, preferred_element_type=F32
            )
            prods.append(jnp.where(slot < used, prod, 0.0))
        for step in range(GROUP):
            spot = out_at(base + step)
            total_ref[spot] = total_ref[spot] + prods[step]
        return carry

    lax.fori_loop(0, (used + GROUP - 1) // GROUP, body, 0)


def product_kernel(flip, carried):
    def kernel(*refs):
        rows_ref, cols_ref, count_ref, index_ref, source_ref, tiles_ref, home_ref = refs[:7]
        if carried:
            kept_ref, out_ref, kept_out_ref, wide_ref, sum_ref, sem = refs[7:]
            kept_copy = pltpu.make_async_copy(kept_ref, kept_out_ref, sem)
            kept_copy.start()
        else:
            out_ref, wide_ref, sum_ref = refs[7:]
        sum_ref[...] = jnp.zeros_like(sum_ref)
        unpack_source(source_ref, wide_ref)
        own_row = lambda slot: rows_ref[0, 0, slot]
        own_col = lambda slot: cols_ref[0, 0, slot]
        home_row = lambda slot: index_ref[0, slot]
        home_col = lambda slot: index_ref[1, slot]
        if flip:
            own_in, own_out, home_in, home_out = own_row, own_col, home_row, home_col
        else:
            own_in, own_out, home_in, home_out = own_col, own_row, home_col, home_row
        add_tiles(own_in, own_out, count_ref[0, 0], wide_ref, sum_ref, tiles_ref, flip)
        add_tiles(home_in, home_out, index_ref[2, 0], wide_ref, sum_ref, home_ref, flip)
        pack_total(sum_ref, out_ref)
        if carried:
            kept_copy.wait()

    return kernel


def product(rows, cols, count, index, source, tiles, home, flip, kept=None):
    wide = (source.shape[0] // 4, 32, 256)
    operands = [rows, cols, count, index, near(source), near(tiles), home]
    out_shape, out_specs = [OUT(source.shape, BF16)], [vmem()]
    scratch = [pltpu.VMEM(wide, BF16), pltpu.VMEM(wide, F32)]
    if kept is not None:
        operands.append(near(kept))
        out_shape.append(jax.ShapeDtypeStruct(kept.shape, kept.dtype))
        out_specs.append(pl.BlockSpec(memory_space=pltpu.HBM))
        scratch.append(pltpu.SemaphoreType.DMA)
    return pl.pallas_call(
        product_kernel(flip, kept is not None),
        compiler_params=SMALL,
        out_shape=out_shape,
        in_specs=[smem()] * 4 + [vmem()] * (len(operands) - 4),
        out_specs=out_specs,
        scratch_shapes=scratch,
    )(*operands)


def load_kernel(count_ref, tiles_ref, out_ref, sems):
    used = count_ref[0, 0]

    def copy(slot):
        return pltpu.make_async_copy(tiles_ref.at[slot], out_ref.at[slot], sems.at[slot])

    def start(slot, carry):
        copy(slot).start()
        return carry

    def wait(slot, carry):
        copy(slot).wait()
        return carry

    lax.fori_loop(0, used, start, 0)
    lax.fori_loop(0, used, wait, 0)


def load_tiles(count, tiles):
    return pl.pallas_call(
        load_kernel,
        compiler_params=SMALL,
        out_shape=OUT(tiles.shape, tiles.dtype),
        in_specs=[smem(), pl.BlockSpec(memory_space=pltpu.HBM)],
        out_specs=vmem(),
        scratch_shapes=[pltpu.SemaphoreType.DMA((tiles.shape[0],))],
    )(count, tiles)


def sum_chunks(received_ref):
    parts = [received_ref[chunk].astype(F32) for chunk in range(received_ref.shape[0])]
    while len(parts) > 1:
        parts = [parts[k] + parts[k + 1] for k in range(0, len(parts), 2)]
    return parts[0]


def store_shard(out_ref, wide):
    out_ref[0:16, :] = wide[:, 0:64]
    out_ref[16:32, :] = pltpu.roll(wide, 64, 1)[:, 0:64]


def middle_kernel(received_ref, degree_ref, out_ref, copies_ref):
    wide = sum_chunks(received_ref) * shard_scale(degree_ref, lax.axis_index("col"))
    store_shard(out_ref, wide)
    packed = wide.astype(BF16)
    for copy in range(copies_ref.shape[0]):
        copies_ref[copy] = packed


def last_kernel(received_ref, degree_ref, out_ref):
    wide = sum_chunks(received_ref) * shard_scale(degree_ref, lax.axis_index("row"))
    store_shard(out_ref, wide)


def exchange(chunks, axis):
    return lax.all_to_all(chunks, axis, 0, 0, tiled=True)


def partner(block):
    count = lax.axis_size("col")
    return lax.ppermute(block, "col", [(k, k ^ (count // 2)) for k in range(count)])


def shards(
    vectors,
    row_degree,
    col_degree,
    tiles,
    tile_rows,
    tile_cols,
    tile_counts,
    lent_tiles,
    lent_rows,
    lent_cols,
    lent_counts,
):
    own = load_tiles(tile_counts, far(tiles.reshape(tiles.shape[2:])))
    lent = lent_tiles.reshape(lent_tiles.shape[2:])
    lents = lent.shape[0]
    tile_rows = far(tile_rows)
    tile_cols = far(tile_cols)
    row_lines = near(row_degree.reshape(-1, 128))
    col_lines = col_degree.reshape(-1, 128)
    row_size, col_size = lax.axis_size("row"), lax.axis_size("col")
    chunk = (16, 128)

    index = jnp.stack(
        [
            lent_rows.reshape(-1),
            lent_cols.reshape(-1),
            jnp.broadcast_to(lent_counts.reshape(1), (lents,)),
        ]
    )
    home = near(partner(lent))
    home_index = partner(index)
    copies = pl.pallas_call(
        pack_kernel,
        compiler_params=SMALL,
        out_shape=OUT((row_size,) + chunk, BF16),
        in_specs=[vmem(), vmem()],
        out_specs=vmem(),
    )(far(vectors.T), far(col_lines))
    source = exchange(copies, "row")
    (partial_value,) = product(
        tile_rows, tile_cols, tile_counts, home_index, source, own, home, False
    )
    first_near, middle_copies = pl.pallas_call(
        middle_kernel,
        compiler_params=SMALL,
        out_shape=(OUT((32, 64), F32), OUT((col_size,) + chunk, BF16)),
        in_specs=[vmem(), vmem()],
        out_specs=(vmem(), vmem()),
    )(near(exchange(partial_value, "col")), row_lines)
    middle = exchange(middle_copies, "col")
    partial_back, first = product(
        tile_rows, tile_cols, tile_counts, home_index, middle, own, home, True, first_near
    )
    second = pl.pallas_call(
        last_kernel,
        compiler_params=SMALL,
        out_shape=jax.ShapeDtypeStruct((32, 64), F32),
        in_specs=[vmem(), vmem()],
        out_specs=vmem(),
    )(near(exchange(partial_back, "row")), near(col_lines))
    return (first.T, second.T)


def solution(mesh):
    return jax.shard_map(
        shards,
        mesh=mesh,
        in_specs=(
            P(("col", "row"), None),
            P("row"),
            P("col"),
            P("row", "col", None, None, None),
            P("row", "col", None),
            P("row", "col", None),
            P("row", "col"),
            P("row", "col", None, None, None),
            P("row", "col", None),
            P("row", "col", None),
            P("row", "col"),
        ),
        out_specs=(P(("row", "col"), None), P(("col", "row"), None)),
        check_vma=False,
    )
```

```python
import jax
import jax.numpy as jnp
from jax import lax
from jax.experimental import pallas as pl
from jax.experimental.pallas import tpu as pltpu
from jax.sharding import PartitionSpec as P

GROUP = 8
SMALL = pltpu.CompilerParams(vmem_limit_bytes=4 * 1024 * 1024)
F32 = jnp.float32
BF16 = jnp.bfloat16


def vmem():
    return pl.BlockSpec(memory_space=pltpu.VMEM)


def smem():
    return pl.BlockSpec(memory_space=pltpu.SMEM)


def OUT(shape, dtype):
    return pltpu.VMEM(shape, dtype)


def near(array):
    return pltpu.with_memory_space_constraint(array, pltpu.VMEM)


def far(array):
    return pltpu.with_memory_space_constraint(array, pltpu.HBM)


def low_lanes(shape):
    return lax.broadcasted_iota(jnp.int32, shape, len(shape) - 1) < shape[-1] // 2


def shard_scale(degree_ref, place):
    line = degree_ref[pl.ds(place // 2, 1), :]
    turned = pltpu.roll(line, 64, 1)
    first_half = place % 2 == 0
    low = low_lanes(line.shape)
    both = jnp.where(low == first_half, line, turned)
    return lax.rsqrt(both)


def pack_kernel(
    vectors_ref, degree_ref, lent_rows_ref, lent_cols_ref, lent_count_ref, out_ref, index_ref
):
    index_ref[0:1, :] = lent_rows_ref[0]
    index_ref[1:2, :] = lent_cols_ref[0]
    index_ref[2:3, :] = jnp.full((1, index_ref.shape[1]), lent_count_ref[0, 0], jnp.int32)
    scale = shard_scale(degree_ref, lax.axis_index("row"))
    values = vectors_ref[...].astype(F32)
    half = values.shape[0] // 2
    wide = jnp.concatenate([values[:half], values[half:]], axis=1) * scale
    packed = wide.astype(BF16)
    for copy in range(out_ref.shape[0]):
        out_ref[copy] = packed


def unpack_source(source_ref, wide_ref):
    low = low_lanes((16, 128))
    for pair in range(source_ref.shape[0] // 2):
        even = source_ref[2 * pair].astype(F32)
        odd = source_ref[2 * pair + 1].astype(F32)
        top = jnp.where(low, even, pltpu.roll(odd, 64, 1))
        bottom = jnp.where(low, pltpu.roll(even, 64, 1), odd)
        lanes = slice(128 * (pair % 2), 128 * (pair % 2) + 128)
        wide_ref[pair // 2, 0:16, lanes] = top.astype(BF16)
        wide_ref[pair // 2, 16:32, lanes] = bottom.astype(BF16)


def pack_total(total_ref, out_ref):
    low = low_lanes((16, 128))
    for pair in range(out_ref.shape[0] // 2):
        lanes = slice(128 * (pair % 2), 128 * (pair % 2) + 128)
        top = total_ref[pair // 2, 0:16, lanes]
        bottom = total_ref[pair // 2, 16:32, lanes]
        even = jnp.where(low, top, pltpu.roll(bottom, 64, 1))
        odd = jnp.where(low, pltpu.roll(top, 64, 1), bottom)
        out_ref[2 * pair] = even.astype(out_ref.dtype)
        out_ref[2 * pair + 1] = odd.astype(out_ref.dtype)


def add_tiles(in_at, out_at, used, wide_ref, total_ref, tiles_ref, flip):
    contract = (((1,), (0,)), ((), ())) if flip else (((1,), (1,)), ((), ()))

    def body(group, carry):
        base = group * GROUP
        prods = []
        for step in range(GROUP):
            slot = base + step
            prod = lax.dot_general(
                wide_ref[in_at(slot)], tiles_ref[slot], contract, preferred_element_type=F32
            )
            prods.append(jnp.where(slot < used, prod, 0.0))
        for step in range(GROUP):
            spot = out_at(base + step)
            total_ref[spot] = total_ref[spot] + prods[step]
        return carry

    lax.fori_loop(0, (used + GROUP - 1) // GROUP, body, 0)


def product_kernel(flip, carried):
    def kernel(*refs):
        rows_ref, cols_ref, count_ref, index_ref, source_ref, tiles_ref, home_ref = refs[:7]
        if carried:
            kept_ref, out_ref, kept_out_ref, wide_ref, sum_ref, sem = refs[7:]
            kept_copy = pltpu.make_async_copy(kept_ref, kept_out_ref, sem)
            kept_copy.start()
        else:
            out_ref, wide_ref, sum_ref = refs[7:]
        sum_ref[...] = jnp.zeros_like(sum_ref)
        unpack_source(source_ref, wide_ref)
        own_row = lambda slot: rows_ref[0, 0, slot]
        own_col = lambda slot: cols_ref[0, 0, slot]
        home_row = lambda slot: index_ref[0, slot]
        home_col = lambda slot: index_ref[1, slot]
        if flip:
            own_in, own_out, home_in, home_out = own_row, own_col, home_row, home_col
        else:
            own_in, own_out, home_in, home_out = own_col, own_row, home_col, home_row
        add_tiles(own_in, own_out, count_ref[0, 0], wide_ref, sum_ref, tiles_ref, flip)
        add_tiles(home_in, home_out, index_ref[2, 0], wide_ref, sum_ref, home_ref, flip)
        pack_total(sum_ref, out_ref)
        if carried:
            kept_copy.wait()

    return kernel


def product(rows, cols, count, index, source, tiles, home, flip, kept=None):
    wide = (source.shape[0] // 4, 32, 256)
    operands = [rows, cols, count, index, near(source), near(tiles), home]
    out_shape, out_specs = [OUT(source.shape, BF16)], [vmem()]
    scratch = [pltpu.VMEM(wide, BF16), pltpu.VMEM(wide, F32)]
    if kept is not None:
        operands.append(near(kept))
        out_shape.append(jax.ShapeDtypeStruct(kept.shape, kept.dtype))
        out_specs.append(pl.BlockSpec(memory_space=pltpu.HBM))
        scratch.append(pltpu.SemaphoreType.DMA)
    return pl.pallas_call(
        product_kernel(flip, kept is not None),
        compiler_params=SMALL,
        out_shape=out_shape,
        in_specs=[smem()] * 4 + [vmem()] * (len(operands) - 4),
        out_specs=out_specs,
        scratch_shapes=scratch,
    )(*operands)


def load_kernel(count_ref, tiles_ref, out_ref, sems):
    used = count_ref[0, 0]

    def copy(slot):
        return pltpu.make_async_copy(tiles_ref.at[slot], out_ref.at[slot], sems.at[slot])

    def start(slot, carry):
        copy(slot).start()
        return carry

    def wait(slot, carry):
        copy(slot).wait()
        return carry

    lax.fori_loop(0, used, start, 0)
    lax.fori_loop(0, used, wait, 0)


def load_tiles(count, tiles):
    return pl.pallas_call(
        load_kernel,
        compiler_params=SMALL,
        out_shape=OUT(tiles.shape, tiles.dtype),
        in_specs=[smem(), pl.BlockSpec(memory_space=pltpu.HBM)],
        out_specs=vmem(),
        scratch_shapes=[pltpu.SemaphoreType.DMA((tiles.shape[0],))],
    )(count, tiles)


def sum_chunks(received_ref):
    parts = [received_ref[chunk].astype(F32) for chunk in range(received_ref.shape[0])]
    while len(parts) > 1:
        parts = [parts[k] + parts[k + 1] for k in range(0, len(parts), 2)]
    return parts[0]


def store_shard(out_ref, wide):
    out_ref[0:16, :] = wide[:, 0:64]
    out_ref[16:32, :] = pltpu.roll(wide, 64, 1)[:, 0:64]


def middle_kernel(received_ref, degree_ref, out_ref, copies_ref):
    wide = sum_chunks(received_ref) * shard_scale(degree_ref, lax.axis_index("col"))
    store_shard(out_ref, wide)
    packed = wide.astype(BF16)
    for copy in range(copies_ref.shape[0]):
        copies_ref[copy] = packed


def last_kernel(received_ref, degree_ref, out_ref):
    wide = sum_chunks(received_ref) * shard_scale(degree_ref, lax.axis_index("row"))
    store_shard(out_ref, wide)


def exchange(chunks, axis):
    return lax.all_to_all(chunks, axis, 0, 0, tiled=True)


def partner(block):
    count = lax.axis_size("col")
    return lax.ppermute(block, "col", [(k, k ^ (count // 2)) for k in range(count)])


def shards(
    vectors,
    row_degree,
    col_degree,
    tiles,
    tile_rows,
    tile_cols,
    tile_counts,
    lent_tiles,
    lent_rows,
    lent_cols,
    lent_counts,
):
    own = load_tiles(tile_counts, far(tiles.reshape(tiles.shape[2:])))
    lent = lent_tiles.reshape(lent_tiles.shape[2:])
    lents = lent.shape[0]
    tile_rows = far(tile_rows)
    tile_cols = far(tile_cols)
    row_lines = near(row_degree.reshape(-1, 128))
    col_lines = col_degree.reshape(-1, 128)
    row_size, col_size = lax.axis_size("row"), lax.axis_size("col")
    chunk = (16, 128)

    home = near(partner(lent))
    copies, index = pl.pallas_call(
        pack_kernel,
        compiler_params=SMALL,
        out_shape=(OUT((row_size,) + chunk, BF16), OUT((3, lents), jnp.int32)),
        in_specs=[vmem()] * 4 + [smem()],
        out_specs=(vmem(), vmem()),
    )(far(vectors.T), far(col_lines), far(lent_rows), far(lent_cols), lent_counts)
    home_index = partner(index)
    source = exchange(copies, "row")
    (partial_value,) = product(
        tile_rows, tile_cols, tile_counts, home_index, source, own, home, False
    )
    first_near, middle_copies = pl.pallas_call(
        middle_kernel,
        compiler_params=SMALL,
        out_shape=(OUT((32, 64), F32), OUT((col_size,) + chunk, BF16)),
        in_specs=[vmem(), vmem()],
        out_specs=(vmem(), vmem()),
    )(near(exchange(partial_value, "col")), row_lines)
    middle = exchange(middle_copies, "col")
    partial_back, first = product(
        tile_rows, tile_cols, tile_counts, home_index, middle, own, home, True, first_near
    )
    second = pl.pallas_call(
        last_kernel,
        compiler_params=SMALL,
        out_shape=jax.ShapeDtypeStruct((32, 64), F32),
        in_specs=[vmem(), vmem()],
        out_specs=vmem(),
    )(near(exchange(partial_back, "row")), near(col_lines))
    return (first.T, second.T)


def solution(mesh):
    return jax.shard_map(
        shards,
        mesh=mesh,
        in_specs=(
            P(("col", "row"), None),
            P("row"),
            P("col"),
            P("row", "col", None, None, None),
            P("row", "col", None),
            P("row", "col", None),
            P("row", "col"),
            P("row", "col", None, None, None),
            P("row", "col", None),
            P("row", "col", None),
            P("row", "col"),
        ),
        out_specs=(P(("row", "col"), None), P(("col", "row"), None)),
        check_vma=False,
    )
```

```python
import jax
import jax.numpy as jnp
from jax import lax
from jax.experimental import pallas as pl
from jax.experimental.pallas import tpu as pltpu
from jax.sharding import PartitionSpec as P

GROUP = 8
SMALL = pltpu.CompilerParams(vmem_limit_bytes=4 * 1024 * 1024)
F32 = jnp.float32
BF16 = jnp.bfloat16


def vmem():
    return pl.BlockSpec(memory_space=pltpu.VMEM)


def smem():
    return pl.BlockSpec(memory_space=pltpu.SMEM)


def OUT(shape, dtype):
    return pltpu.VMEM(shape, dtype)


def near(array):
    return pltpu.with_memory_space_constraint(array, pltpu.VMEM)


def far(array):
    return pltpu.with_memory_space_constraint(array, pltpu.HBM)


def low_lanes(shape):
    return lax.broadcasted_iota(jnp.int32, shape, len(shape) - 1) < shape[-1] // 2


def shard_scale(degree_ref, place):
    line = degree_ref[pl.ds(place // 2, 1), :]
    turned = pltpu.roll(line, 64, 1)
    first_half = place % 2 == 0
    low = low_lanes(line.shape)
    both = jnp.where(low == first_half, line, turned)
    return lax.rsqrt(both)


def pack_kernel(vectors_ref, degree_ref, out_ref):
    scale = shard_scale(degree_ref, lax.axis_index("row"))
    values = vectors_ref[...].astype(F32)
    half = values.shape[0] // 2
    wide = jnp.concatenate([values[:half], values[half:]], axis=1) * scale
    packed = wide.astype(BF16)
    for copy in range(out_ref.shape[0]):
        out_ref[copy] = packed


def unpack_source(source_ref, wide_ref):
    low = low_lanes((16, 128))
    for pair in range(source_ref.shape[0] // 2):
        even = source_ref[2 * pair].astype(F32)
        odd = source_ref[2 * pair + 1].astype(F32)
        top = jnp.where(low, even, pltpu.roll(odd, 64, 1))
        bottom = jnp.where(low, pltpu.roll(even, 64, 1), odd)
        lanes = slice(128 * (pair % 2), 128 * (pair % 2) + 128)
        wide_ref[pair // 2, 0:16, lanes] = top.astype(BF16)
        wide_ref[pair // 2, 16:32, lanes] = bottom.astype(BF16)


def pack_total(total_ref, out_ref):
    low = low_lanes((16, 128))
    for pair in range(out_ref.shape[0] // 2):
        lanes = slice(128 * (pair % 2), 128 * (pair % 2) + 128)
        top = total_ref[pair // 2, 0:16, lanes]
        bottom = total_ref[pair // 2, 16:32, lanes]
        even = jnp.where(low, top, pltpu.roll(bottom, 64, 1))
        odd = jnp.where(low, pltpu.roll(top, 64, 1), bottom)
        out_ref[2 * pair] = even.astype(out_ref.dtype)
        out_ref[2 * pair + 1] = odd.astype(out_ref.dtype)


def add_tiles(in_at, out_at, used, wide_ref, total_ref, tiles_ref, flip):
    contract = (((1,), (0,)), ((), ())) if flip else (((1,), (1,)), ((), ()))

    def body(group, carry):
        base = group * GROUP
        prods = []
        for step in range(GROUP):
            slot = base + step
            prod = lax.dot_general(
                wide_ref[in_at(slot)], tiles_ref[slot], contract, preferred_element_type=F32
            )
            prods.append(jnp.where(slot < used, prod, 0.0))
        for step in range(GROUP):
            spot = out_at(base + step)
            total_ref[spot] = total_ref[spot] + prods[step]
        return carry

    lax.fori_loop(0, (used + GROUP - 1) // GROUP, body, 0)


def own_kernel(rows_ref, cols_ref, count_ref, source_ref, tiles_ref, sum_ref, wide_ref):
    sum_ref[...] = jnp.zeros_like(sum_ref)
    unpack_source(source_ref, wide_ref)
    add_tiles(
        lambda slot: cols_ref[0, 0, slot],
        lambda slot: rows_ref[0, 0, slot],
        count_ref[0, 0],
        wide_ref,
        sum_ref,
        tiles_ref,
        False,
    )


def home_kernel(index_ref, wide_ref, home_ref, own_sum_ref, out_ref, sum_ref):
    sum_ref[...] = own_sum_ref[...]
    add_tiles(
        lambda slot: index_ref[1, slot],
        lambda slot: index_ref[0, slot],
        index_ref[2, 0],
        wide_ref,
        sum_ref,
        home_ref,
        False,
    )
    pack_total(sum_ref, out_ref)


def forth(rows, cols, count, index, source, tiles, home):
    wide = (source.shape[0] // 4, 32, 256)
    own_sum, wide_source = pl.pallas_call(
        own_kernel,
        compiler_params=SMALL,
        out_shape=(OUT(wide, F32), OUT(wide, BF16)),
        in_specs=[smem()] * 3 + [vmem()] * 2,
        out_specs=(vmem(), vmem()),
    )(rows, cols, count, near(source), near(tiles))
    return pl.pallas_call(
        home_kernel,
        compiler_params=SMALL,
        out_shape=OUT(source.shape, BF16),
        in_specs=[smem()] + [vmem()] * 3,
        out_specs=vmem(),
        scratch_shapes=[pltpu.VMEM(wide, F32)],
    )(index, near(wide_source), home, near(own_sum))


def back_kernel(
    rows_ref,
    cols_ref,
    count_ref,
    index_ref,
    source_ref,
    tiles_ref,
    home_ref,
    kept_ref,
    out_ref,
    kept_out_ref,
    wide_ref,
    sum_ref,
    sem,
):
    kept_copy = pltpu.make_async_copy(kept_ref, kept_out_ref, sem)
    kept_copy.start()
    sum_ref[...] = jnp.zeros_like(sum_ref)
    unpack_source(source_ref, wide_ref)
    add_tiles(
        lambda slot: rows_ref[0, 0, slot],
        lambda slot: cols_ref[0, 0, slot],
        count_ref[0, 0],
        wide_ref,
        sum_ref,
        tiles_ref,
        True,
    )
    add_tiles(
        lambda slot: index_ref[0, slot],
        lambda slot: index_ref[1, slot],
        index_ref[2, 0],
        wide_ref,
        sum_ref,
        home_ref,
        True,
    )
    pack_total(sum_ref, out_ref)
    kept_copy.wait()


def back(rows, cols, count, index, source, tiles, home, kept):
    wide = (source.shape[0] // 4, 32, 256)
    return pl.pallas_call(
        back_kernel,
        compiler_params=SMALL,
        out_shape=(
            OUT(source.shape, BF16),
            jax.ShapeDtypeStruct(kept.shape, kept.dtype),
        ),
        in_specs=[smem()] * 4 + [vmem()] * 4,
        out_specs=(vmem(), pl.BlockSpec(memory_space=pltpu.HBM)),
        scratch_shapes=[
            pltpu.VMEM(wide, BF16),
            pltpu.VMEM(wide, F32),
            pltpu.SemaphoreType.DMA,
        ],
    )(rows, cols, count, index, near(source), near(tiles), home, near(kept))


def load_kernel(count_ref, tiles_ref, out_ref, sems):
    used = count_ref[0, 0]

    def copy(slot):
        return pltpu.make_async_copy(tiles_ref.at[slot], out_ref.at[slot], sems.at[slot])

    def start(slot, carry):
        copy(slot).start()
        return carry

    def wait(slot, carry):
        copy(slot).wait()
        return carry

    lax.fori_loop(0, used, start, 0)
    lax.fori_loop(0, used, wait, 0)


def load_tiles(count, tiles):
    return pl.pallas_call(
        load_kernel,
        compiler_params=SMALL,
        out_shape=OUT(tiles.shape, tiles.dtype),
        in_specs=[smem(), pl.BlockSpec(memory_space=pltpu.HBM)],
        out_specs=vmem(),
        scratch_shapes=[pltpu.SemaphoreType.DMA((tiles.shape[0],))],
    )(count, tiles)


def sum_chunks(received_ref):
    parts = [received_ref[chunk].astype(F32) for chunk in range(received_ref.shape[0])]
    while len(parts) > 1:
        parts = [parts[k] + parts[k + 1] for k in range(0, len(parts), 2)]
    return parts[0]


def store_shard(out_ref, wide):
    out_ref[0:16, :] = wide[:, 0:64]
    out_ref[16:32, :] = pltpu.roll(wide, 64, 1)[:, 0:64]


def middle_kernel(received_ref, degree_ref, out_ref, copies_ref):
    wide = sum_chunks(received_ref) * shard_scale(degree_ref, lax.axis_index("col"))
    store_shard(out_ref, wide)
    packed = wide.astype(BF16)
    for copy in range(copies_ref.shape[0]):
        copies_ref[copy] = packed


def last_kernel(received_ref, degree_ref, out_ref):
    wide = sum_chunks(received_ref) * shard_scale(degree_ref, lax.axis_index("row"))
    store_shard(out_ref, wide)


def exchange(chunks, axis):
    return lax.all_to_all(chunks, axis, 0, 0, tiled=True)


def partner(block):
    count = lax.axis_size("col")
    return lax.ppermute(block, "col", [(k, k ^ (count // 2)) for k in range(count)])


def shards(
    vectors,
    row_degree,
    col_degree,
    tiles,
    tile_rows,
    tile_cols,
    tile_counts,
    lent_tiles,
    lent_rows,
    lent_cols,
    lent_counts,
):
    own = load_tiles(tile_counts, far(tiles.reshape(tiles.shape[2:])))
    lent = lent_tiles.reshape(lent_tiles.shape[2:])
    lents = lent.shape[0]
    tile_rows = far(tile_rows)
    tile_cols = far(tile_cols)
    row_lines = near(row_degree.reshape(-1, 128))
    col_lines = col_degree.reshape(-1, 128)
    row_size, col_size = lax.axis_size("row"), lax.axis_size("col")
    chunk = (16, 128)

    index = jnp.stack(
        [
            lent_rows.reshape(-1),
            lent_cols.reshape(-1),
            jnp.broadcast_to(lent_counts.reshape(1), (lents,)),
        ]
    )
    home = near(partner(lent))
    home_index = partner(index)
    copies = pl.pallas_call(
        pack_kernel,
        compiler_params=SMALL,
        out_shape=OUT((row_size,) + chunk, BF16),
        in_specs=[vmem(), vmem()],
        out_specs=vmem(),
    )(far(vectors.T), far(col_lines))
    source = exchange(copies, "row")
    partial_value = forth(tile_rows, tile_cols, tile_counts, home_index, source, own, home)
    first_near, middle_copies = pl.pallas_call(
        middle_kernel,
        compiler_params=SMALL,
        out_shape=(OUT((32, 64), F32), OUT((col_size,) + chunk, BF16)),
        in_specs=[vmem(), vmem()],
        out_specs=(vmem(), vmem()),
    )(near(exchange(partial_value, "col")), row_lines)
    middle = exchange(middle_copies, "col")
    partial_back, first = back(
        tile_rows, tile_cols, tile_counts, home_index, middle, own, home, first_near
    )
    second = pl.pallas_call(
        last_kernel,
        compiler_params=SMALL,
        out_shape=jax.ShapeDtypeStruct((32, 64), F32),
        in_specs=[vmem(), vmem()],
        out_specs=vmem(),
    )(near(exchange(partial_back, "row")), near(col_lines))
    return (first.T, second.T)


def solution(mesh):
    return jax.shard_map(
        shards,
        mesh=mesh,
        in_specs=(
            P(("col", "row"), None),
            P("row"),
            P("col"),
            P("row", "col", None, None, None),
            P("row", "col", None),
            P("row", "col", None),
            P("row", "col"),
            P("row", "col", None, None, None),
            P("row", "col", None),
            P("row", "col", None),
            P("row", "col"),
        ),
        out_specs=(P(("row", "col"), None), P(("col", "row"), None)),
        check_vma=False,
    )
```

```python
import jax
import jax.numpy as jnp
from jax import lax
from jax.experimental import pallas as pl
from jax.experimental.pallas import tpu as pltpu
from jax.sharding import PartitionSpec as P

SMALL = pltpu.CompilerParams(vmem_limit_bytes=4 * 1024 * 1024)
F32 = jnp.float32
BF16 = jnp.bfloat16


def vmem():
    return pl.BlockSpec(memory_space=pltpu.VMEM)


def smem():
    return pl.BlockSpec(memory_space=pltpu.SMEM)


def OUT(shape, dtype):
    return pltpu.VMEM(shape, dtype)


def near(array):
    return pltpu.with_memory_space_constraint(array, pltpu.VMEM)


def far(array):
    return pltpu.with_memory_space_constraint(array, pltpu.HBM)


def low_lanes(shape):
    return lax.broadcasted_iota(jnp.int32, shape, len(shape) - 1) < shape[-1] // 2


def shard_scale(degree_ref, place):
    line = degree_ref[pl.ds(place // 2, 1), :]
    turned = pltpu.roll(line, 64, 1)
    first_half = place % 2 == 0
    low = low_lanes(line.shape)
    both = jnp.where(low == first_half, line, turned)
    return lax.rsqrt(both)


def pack_kernel(
    vectors_ref, degree_ref, lent_rows_ref, lent_cols_ref, lent_count_ref, out_ref, index_ref
):
    index_ref[0:1, :] = lent_rows_ref[0]
    index_ref[1:2, :] = lent_cols_ref[0]
    index_ref[2:3, :] = jnp.full((1, index_ref.shape[1]), lent_count_ref[0, 0], jnp.int32)
    scale = shard_scale(degree_ref, lax.axis_index("row"))
    values = vectors_ref[...].astype(F32)
    half = values.shape[0] // 2
    wide = jnp.concatenate([values[:half], values[half:]], axis=1) * scale
    packed = wide.astype(BF16)
    for copy in range(out_ref.shape[0]):
        out_ref[copy] = packed


def unpack_source(source_ref, wide_ref):
    low = low_lanes((16, 128))
    for pair in range(source_ref.shape[0] // 2):
        even = source_ref[2 * pair].astype(F32)
        odd = source_ref[2 * pair + 1].astype(F32)
        top = jnp.where(low, even, pltpu.roll(odd, 64, 1))
        bottom = jnp.where(low, pltpu.roll(even, 64, 1), odd)
        lanes = slice(128 * (pair % 2), 128 * (pair % 2) + 128)
        wide_ref[pair // 2, 0:16, lanes] = top.astype(BF16)
        wide_ref[pair // 2, 16:32, lanes] = bottom.astype(BF16)


def pack_total(total_ref, out_ref):
    low = low_lanes((16, 128))
    for pair in range(out_ref.shape[0] // 2):
        lanes = slice(128 * (pair % 2), 128 * (pair % 2) + 128)
        top = total_ref[pair // 2, 0:16, lanes]
        bottom = total_ref[pair // 2, 16:32, lanes]
        even = jnp.where(low, top, pltpu.roll(bottom, 64, 1))
        odd = jnp.where(low, pltpu.roll(top, 64, 1), bottom)
        out_ref[2 * pair] = even.astype(out_ref.dtype)
        out_ref[2 * pair + 1] = odd.astype(out_ref.dtype)


def add_tiles(in_at, out_at, used, wide_ref, total_ref, tiles_ref, flip):
    contract = (((1,), (0,)), ((), ())) if flip else (((1,), (1,)), ((), ()))

    @pl.when(used > 0)
    def _():
        for slot in range(tiles_ref.shape[0]):
            prod = lax.dot_general(
                wide_ref[in_at(slot)], tiles_ref[slot], contract, preferred_element_type=F32
            )
            spot = out_at(slot)
            total_ref[spot] = total_ref[spot] + jnp.where(slot < used, prod, 0.0)


def product_kernel(flip, carried):
    def kernel(*refs):
        rows_ref, cols_ref, count_ref, index_ref, source_ref, tiles_ref, home_ref = refs[:7]
        if carried:
            kept_ref, out_ref, kept_out_ref, wide_ref, sum_ref, sem = refs[7:]
            kept_copy = pltpu.make_async_copy(kept_ref, kept_out_ref, sem)
            kept_copy.start()
        else:
            out_ref, wide_ref, sum_ref = refs[7:]
        sum_ref[...] = jnp.zeros_like(sum_ref)
        unpack_source(source_ref, wide_ref)
        own_row = lambda slot: rows_ref[0, 0, slot]
        own_col = lambda slot: cols_ref[0, 0, slot]
        home_row = lambda slot: index_ref[0, slot]
        home_col = lambda slot: index_ref[1, slot]
        if flip:
            own_in, own_out, home_in, home_out = own_row, own_col, home_row, home_col
        else:
            own_in, own_out, home_in, home_out = own_col, own_row, home_col, home_row
        add_tiles(own_in, own_out, count_ref[0, 0], wide_ref, sum_ref, tiles_ref, flip)
        add_tiles(home_in, home_out, index_ref[2, 0], wide_ref, sum_ref, home_ref, flip)
        pack_total(sum_ref, out_ref)
        if carried:
            kept_copy.wait()

    return kernel


def product(rows, cols, count, index, source, tiles, home, flip, kept=None):
    wide = (source.shape[0] // 4, 32, 256)
    operands = [rows, cols, count, index, near(source), near(tiles), home]
    out_shape, out_specs = [OUT(source.shape, BF16)], [vmem()]
    scratch = [pltpu.VMEM(wide, BF16), pltpu.VMEM(wide, F32)]
    if kept is not None:
        operands.append(near(kept))
        out_shape.append(jax.ShapeDtypeStruct(kept.shape, kept.dtype))
        out_specs.append(pl.BlockSpec(memory_space=pltpu.HBM))
        scratch.append(pltpu.SemaphoreType.DMA)
    return pl.pallas_call(
        product_kernel(flip, kept is not None),
        compiler_params=SMALL,
        out_shape=out_shape,
        in_specs=[smem()] * 4 + [vmem()] * (len(operands) - 4),
        out_specs=out_specs,
        scratch_shapes=scratch,
    )(*operands)


def load_kernel(count_ref, tiles_ref, out_ref, sems):
    used = count_ref[0, 0]

    def copy(slot):
        return pltpu.make_async_copy(tiles_ref.at[slot], out_ref.at[slot], sems.at[slot])

    def start(slot, carry):
        copy(slot).start()
        return carry

    def wait(slot, carry):
        copy(slot).wait()
        return carry

    lax.fori_loop(0, used, start, 0)
    lax.fori_loop(0, used, wait, 0)


def load_tiles(count, tiles):
    return pl.pallas_call(
        load_kernel,
        compiler_params=SMALL,
        out_shape=OUT(tiles.shape, tiles.dtype),
        in_specs=[smem(), pl.BlockSpec(memory_space=pltpu.HBM)],
        out_specs=vmem(),
        scratch_shapes=[pltpu.SemaphoreType.DMA((tiles.shape[0],))],
    )(count, tiles)


def sum_chunks(received_ref):
    parts = [received_ref[chunk].astype(F32) for chunk in range(received_ref.shape[0])]
    while len(parts) > 1:
        parts = [parts[k] + parts[k + 1] for k in range(0, len(parts), 2)]
    return parts[0]


def store_shard(out_ref, wide):
    out_ref[0:16, :] = wide[:, 0:64]
    out_ref[16:32, :] = pltpu.roll(wide, 64, 1)[:, 0:64]


def middle_kernel(received_ref, degree_ref, out_ref, copies_ref):
    wide = sum_chunks(received_ref) * shard_scale(degree_ref, lax.axis_index("col"))
    store_shard(out_ref, wide)
    packed = wide.astype(BF16)
    for copy in range(copies_ref.shape[0]):
        copies_ref[copy] = packed


def last_kernel(received_ref, degree_ref, out_ref):
    wide = sum_chunks(received_ref) * shard_scale(degree_ref, lax.axis_index("row"))
    store_shard(out_ref, wide)


def exchange(chunks, axis):
    return lax.all_to_all(chunks, axis, 0, 0, tiled=True)


def partner(block):
    count = lax.axis_size("col")
    return lax.ppermute(block, "col", [(k, k ^ (count // 2)) for k in range(count)])


def shards(
    vectors,
    row_degree,
    col_degree,
    tiles,
    tile_rows,
    tile_cols,
    tile_counts,
    lent_tiles,
    lent_rows,
    lent_cols,
    lent_counts,
):
    own = load_tiles(tile_counts, far(tiles.reshape(tiles.shape[2:])))
    lent = lent_tiles.reshape(lent_tiles.shape[2:])
    lents = lent.shape[0]
    tile_rows = far(tile_rows)
    tile_cols = far(tile_cols)
    row_lines = near(row_degree.reshape(-1, 128))
    col_lines = col_degree.reshape(-1, 128)
    row_size, col_size = lax.axis_size("row"), lax.axis_size("col")
    chunk = (16, 128)

    home = near(partner(lent))
    copies, index = pl.pallas_call(
        pack_kernel,
        compiler_params=SMALL,
        out_shape=(OUT((row_size,) + chunk, BF16), OUT((3, lents), jnp.int32)),
        in_specs=[vmem()] * 4 + [smem()],
        out_specs=(vmem(), vmem()),
    )(far(vectors.T), far(col_lines), far(lent_rows), far(lent_cols), lent_counts)
    home_index = partner(index)
    source = exchange(copies, "row")
    (partial_value,) = product(
        tile_rows, tile_cols, tile_counts, home_index, source, own, home, False
    )
    first_near, middle_copies = pl.pallas_call(
        middle_kernel,
        compiler_params=SMALL,
        out_shape=(OUT((32, 64), F32), OUT((col_size,) + chunk, BF16)),
        in_specs=[vmem(), vmem()],
        out_specs=(vmem(), vmem()),
    )(near(exchange(partial_value, "col")), row_lines)
    middle = exchange(middle_copies, "col")
    partial_back, first = product(
        tile_rows, tile_cols, tile_counts, home_index, middle, own, home, True, first_near
    )
    second = pl.pallas_call(
        last_kernel,
        compiler_params=SMALL,
        out_shape=jax.ShapeDtypeStruct((32, 64), F32),
        in_specs=[vmem(), vmem()],
        out_specs=vmem(),
    )(near(exchange(partial_back, "row")), near(col_lines))
    return (first.T, second.T)


def solution(mesh):
    return jax.shard_map(
        shards,
        mesh=mesh,
        in_specs=(
            P(("col", "row"), None),
            P("row"),
            P("col"),
            P("row", "col", None, None, None),
            P("row", "col", None),
            P("row", "col", None),
            P("row", "col"),
            P("row", "col", None, None, None),
            P("row", "col", None),
            P("row", "col", None),
            P("row", "col"),
        ),
        out_specs=(P(("row", "col"), None), P(("col", "row"), None)),
        check_vma=False,
    )
```
